256 devices in a mesh: row: 32 (over y, x, z_lo), col: 8 (over z_hi, core).
Axes of the slice: x: 4, y: 4, z: 8 (z_hi: 4, z_lo: 2; z = z_hi * 2 + z_lo), core: 2. Of those that a mesh axis runs over, the one named last changes fastest.
Arguments:
- token_keys: bfloat16 [131072, 768], P(('row', 'col')), may hold values from -6 to 6
- token_values: bfloat16 [131072, 768], P(('row', 'col')), may hold values from -6 to 6
- token_queries: bfloat16 [131072, 768], P(('row', 'col')), may hold values from -6 to 6
- step_rates: float32 [131072], P(('row', 'col')), may hold values from 5e-05 to 0.0005
- fast_gate: float32 [768, 768], P('col'), may hold values from -0.21875 to 0.21875
- fast_up: float32 [768, 768], P('col'), may hold values from -0.21875 to 0.21875
- fast_down: float32 [768, 768], P('col'), may hold values from -0.21875 to 0.21875
- norm_gain: float32 [768], replicated, may hold values from 0.25 to 1.75
- proj_query: bfloat16 [768, 768], replicated, may hold values from -0.21875 to 0.21875
- proj_key: bfloat16 [768, 768], replicated, may hold values from -0.21875 to 0.21875
- proj_value: bfloat16 [768, 768], replicated, may hold values from -0.21875 to 0.21875
- head_temper: float32 [12], replicated, may hold values from 1 to 12
Outputs:
- attended: bfloat16 [131072, 768], P(('row', 'col'))
- new_gate: float32 [768, 768], P('col')
- new_up: float32 [768, 768], P('col')
- new_down: float32 [768, 768], P('col')
The draws below stay inside these ranges and needn't reach their ends.
All inputs are finite; a program needn't handle non-finite values.
Results may differ from the reference program's by a relative error of at most 0.035.
The reference program's roundings to bfloat16 on the way count: a program that leaves them out, or rounds other values in their place, can miss the bound.
Values may be sent and summed in bfloat16 or wider, within the bound.
No kernel may reach another device: no remote copies, remote signals or barrier semaphores. Data moves between devices by JAX's collectives and lax.ppermute only.
A program may use at most 64 MiB of HBM per device.

```python
import math
import jax
import jax.numpy as jnp
from jax import lax

D = 768
H = 768
HEADS = 12
TOK_DEV = 512
HALF = 256
TOKENS = 131072


def draw_head_temper(key, part):
    first = jax.random.fold_in(key, 11)
    modest = jnp.exp(jax.random.uniform(first, (HEADS,), jnp.float32, jnp.log(1.0), jnp.log(4.0)))
    return modest


def levels(rng, dims, split, least, top_value):
    factor_of = 1.0
    for dim, shards_of in split:
        heights = jax.random.uniform(jax.random.fold_in(jax.random.fold_in(rng, 6), dim), (shards_of,), jnp.float32, least / len(split), top_value / len(split))
        factor_of = factor_of * jnp.repeat(jnp.exp(heights), dims[dim] // shards_of).reshape((-1,) + (1,) * (len(dims) - 1 - dim))
    return factor_of


def noise(rng, dims, scale, reach, shards=(), kind=jnp.bfloat16):
    entries = jax.random.normal(rng, dims, jnp.float32) * scale
    if len(shards) > 0:
        entries = levels(rng, dims, shards, -0.22, 0.18) * entries
    return jnp.clip(entries, min=-reach, max=reach).astype(kind)


def setup_inputs(seed: int = 0) -> dict:
    splits = jax.random.split(jax.random.key(seed), 13)
    token_keys = noise(splits[0], (TOKENS, D), 1.0, 6.0, ((0, 256),))
    token_values = noise(splits[1], (TOKENS, D), 1.0, 6.0, ((0, 256),))
    token_queries = noise(splits[2], (TOKENS, D), 1.0, 6.0, ((0, 256),))
    step_rates = jnp.clip(jnp.exp(math.log(0.0005) - 2.3025852 * jax.random.uniform(splits[3], (TOKENS,), jnp.float32) ** levels(splits[3], (TOKENS,), ((0, 256),), -0.2, 0.2)), 4.999999873689376e-05, 0.0005)
    fast_gate = noise(splits[4], (H, D), D ** -0.5, 0.21875, ((0, 8),), jnp.float32)
    fast_up = noise(splits[5], (H, D), D ** -0.5, 0.21875, ((0, 8),), jnp.float32)
    fast_down = noise(splits[6], (D, H), H ** -0.5, 0.21875, ((0, 8),), jnp.float32)
    norm_gain = jnp.clip(1.0 + 0.15 * jax.random.normal(splits[7], (D,), jnp.float32), 0.25, 1.75)
    proj_query = noise(splits[8], (D, D), D ** -0.5, 0.21875)
    proj_key = noise(splits[9], (D, D), D ** -0.5, 0.21875)
    proj_value = noise(splits[10], (D, D), D ** -0.5, 0.21875)
    head_temper = draw_head_temper(jax.random.fold_in(splits[12], 71), 0)
    return {"token_keys": token_keys, "token_values": token_values, "token_queries": token_queries, "step_rates": step_rates, "fast_gate": fast_gate, "fast_up": fast_up, "fast_down": fast_down, "norm_gain": norm_gain, "proj_query": proj_query, "proj_key": proj_key, "proj_value": proj_value, "head_temper": head_temper}


EPS_NORM = 1e-06

def dot_rows(left, right):
    return lax.dot_general(left, right, (((1,), (1,)), ((), ())), preferred_element_type=jnp.float32)

def dot_cols(left, right):
    return lax.dot_general(left, right, (((0,), (0,)), ((), ())), preferred_element_type=jnp.float32)

def fast_gradients(token_keys, token_values, step_rates, gate_b, up_b, down_b):
    pre_gate = dot_rows(token_keys, gate_b)
    pre_up = dot_rows(token_keys, up_b)
    sigmoid_gate = jax.nn.sigmoid(pre_gate)
    hidden = (pre_gate * sigmoid_gate * pre_up).astype(jnp.bfloat16)
    d_output = (-step_rates[:, None] * token_values.astype(jnp.float32)).astype(jnp.bfloat16)
    d_hidden = jnp.dot(d_output, down_b, preferred_element_type=jnp.float32)
    d_up = (d_hidden * pre_gate * sigmoid_gate).astype(jnp.bfloat16)
    d_gate = (d_hidden * pre_up * sigmoid_gate * (1.0 + pre_gate * (1.0 - sigmoid_gate))).astype(jnp.bfloat16)
    return (dot_cols(d_gate, token_keys), dot_cols(d_up, token_keys), dot_cols(d_output, hidden))

def renorm(weight, gradient):
    moved = weight - gradient
    keep = jnp.sqrt(lax.optimization_barrier(jnp.sum(weight * weight, axis=1, keepdims=True)))
    return moved * keep * lax.rsqrt(lax.optimization_barrier(jnp.sum(moved * moved, axis=1, keepdims=True)) + EPS_NORM)

def fast_apply(token_queries, gate_b, up_b, down_b):
    pre_gate = dot_rows(token_queries, gate_b)
    pre_up = dot_rows(token_queries, up_b)
    mixed = (pre_gate * jax.nn.sigmoid(pre_gate) * pre_up).astype(jnp.bfloat16)
    return dot_rows(mixed, down_b)

def normed_rows(fast_out, norm_gain):
    inverse = lax.rsqrt(lax.optimization_barrier(jnp.mean(fast_out * fast_out, axis=1, keepdims=True)) + EPS_NORM)
    return (fast_out * inverse * norm_gain[None, :]).astype(jnp.bfloat16)

def head_norm(projected, heads):
    count, features = projected.shape
    shaped = projected.reshape(count, heads, features // heads)
    shaped = shaped * lax.rsqrt(lax.optimization_barrier(jnp.mean(shaped * shaped, axis=2, keepdims=True)) + EPS_NORM)
    return shaped.reshape(count, features).astype(jnp.bfloat16)

def attend(q_rows, k_rows, v_rows, head_temper, half_span):
    heads = head_temper.shape[0]
    head_size = q_rows.shape[1] // heads
    query_count = q_rows.shape[0]
    key_count = k_rows.shape[0]
    offset = jnp.arange(key_count)[None, :] - half_span - jnp.arange(query_count)[:, None]
    inside = jnp.abs(offset) <= half_span

    def one_head(head):
        start = (head * head_size).astype(jnp.int32)
        query_h = lax.dynamic_slice_in_dim(q_rows, start, head_size, 1)
        key_h = lax.dynamic_slice_in_dim(k_rows, start, head_size, 1)
        value_h = lax.dynamic_slice_in_dim(v_rows, start, head_size, 1)
        scores = dot_rows(query_h, key_h) * (head_temper[head] / math.sqrt(head_size))
        scores = jnp.where(inside, scores, -1e+30)
        highest = lax.optimization_barrier(jnp.max(scores, axis=1, keepdims=True))
        weights = jnp.exp(scores - highest)
        weights = weights / lax.optimization_barrier(jnp.sum(weights, axis=1, keepdims=True))
        return jnp.dot(weights.astype(jnp.bfloat16), value_h, preferred_element_type=jnp.float32)
    stacked = lax.map(one_head, jnp.arange(heads, dtype=jnp.int32))
    return jnp.transpose(stacked, (1, 0, 2)).reshape(query_count, heads * head_size)

def reference(token_keys, token_values, token_queries, step_rates, fast_gate, fast_up, fast_down, norm_gain, proj_query, proj_key, proj_value, head_temper):
    blocks = TOKENS // TOK_DEV
    gate_b = fast_gate.astype(jnp.bfloat16)
    up_b = fast_up.astype(jnp.bfloat16)
    down_b = fast_down.astype(jnp.bfloat16)
    key_blocks = token_keys.reshape(blocks, TOK_DEV, D)
    value_blocks = token_values.reshape(blocks, TOK_DEV, D)
    rate_blocks = step_rates.reshape(blocks, TOK_DEV)

    def accumulate(carry, block_in):
        parts = fast_gradients(block_in[0], block_in[1], block_in[2], gate_b, up_b, down_b)
        return ((carry[0] + parts[0], carry[1] + parts[1], carry[2] + parts[2]), None)
    start_sums = (jnp.zeros((H, D), jnp.float32), jnp.zeros((H, D), jnp.float32), jnp.zeros((D, H), jnp.float32))
    sums, unused = lax.scan(accumulate, start_sums, (key_blocks, value_blocks, rate_blocks))
    new_gate = renorm(fast_gate, sums[0])
    new_up = renorm(fast_up, sums[1])
    new_down = renorm(fast_down, sums[2])
    fast_out = fast_apply(token_queries, new_gate.astype(jnp.bfloat16), new_up.astype(jnp.bfloat16), new_down.astype(jnp.bfloat16))
    normed = normed_rows(fast_out, norm_gain)
    query_n = head_norm(jnp.dot(normed, proj_query, preferred_element_type=jnp.float32), HEADS)
    key_n = head_norm(jnp.dot(normed, proj_key, preferred_element_type=jnp.float32), HEADS)
    value_b = jnp.dot(normed, proj_value, preferred_element_type=jnp.float32).astype(jnp.bfloat16)
    key_pad = jnp.concatenate([key_n[TOKENS - HALF:], key_n, key_n[:HALF]], axis=0)
    value_pad = jnp.concatenate([value_b[TOKENS - HALF:], value_b, value_b[:HALF]], axis=0)

    def one_block(block):
        start = (block * TOK_DEV).astype(jnp.int32)
        q_rows = lax.dynamic_slice_in_dim(query_n, start, TOK_DEV, 0)
        k_rows = lax.dynamic_slice_in_dim(key_pad, start, TOK_DEV + 2 * HALF, 0)
        v_rows = lax.dynamic_slice_in_dim(value_pad, start, TOK_DEV + 2 * HALF, 0)
        return attend(q_rows, k_rows, v_rows, head_temper, HALF)
    attended = lax.map(one_block, jnp.arange(blocks, dtype=jnp.int32))
    return (attended.reshape(TOKENS, D).astype(jnp.bfloat16), new_gate, new_up, new_down)
```

```python
import math

import jax
import jax.numpy as jnp
from jax import lax
from jax.sharding import PartitionSpec as P

EPS_NORM = 1e-06
NX, NY, NZ = 4, 4, 8
ALL = ("row", "col")


def device_of(x, y, z, c):
    x, y, z = x % NX, y % NY, z % NZ
    return ((y * NX + x) * 2 + z % 2) * 8 + (z // 2) * 2 + c


def places():
    return [
        (x, y, z, c) for x in range(NX) for y in range(NY) for z in range(NZ) for c in range(2)
    ]


def pairs(target):
    return [(device_of(*p), device_of(*target(*p))) for p in places()]


def groups(key):
    found = {}
    for p in places():
        name, order = key(*p)
        found.setdefault(name, []).append((order, device_of(*p)))
    return [[device for _, device in sorted(members)] for members in found.values()]


def exchange(blocks, group):
    return lax.all_to_all(blocks, ALL, 0, 0, axis_index_groups=group, tiled=True)


def spread(block, count):
    return jnp.broadcast_to(block[None], (count,) + block.shape)


def padded_2(cells, sides, width):
    for axis, dim in sides:
        count = lax.axis_size(axis)
        head = lax.slice_in_dim(cells, 0, width, axis=dim)
        tail = lax.slice_in_dim(cells, cells.shape[dim] - width, cells.shape[dim], axis=dim)
        cells = jnp.concatenate(
            [
                lax.ppermute(tail, axis, [(i, (i + 1) % count) for i in range(count)]),
                cells,
                lax.ppermute(head, axis, [((i + 1) % count, i) for i in range(count)]),
            ],
            axis=dim,
        )
    return cells


def dot_rows(left, right):
    return lax.dot_general(
        left, right, (((1,), (1,)), ((), ())), preferred_element_type=jnp.float32
    )


def dot_cols(left, right):
    return lax.dot_general(
        left, right, (((0,), (0,)), ((), ())), preferred_element_type=jnp.float32
    )


def fast_gradients(token_keys, token_values, step_rates, gate_b, up_b, down_b):
    pre_gate = dot_rows(token_keys, gate_b)
    pre_up = dot_rows(token_keys, up_b)
    sigmoid_gate = jax.nn.sigmoid(pre_gate)
    hidden = (pre_gate * sigmoid_gate * pre_up).astype(jnp.bfloat16)
    d_output = (-step_rates[:, None] * token_values.astype(jnp.float32)).astype(jnp.bfloat16)
    d_hidden = jnp.dot(d_output, down_b, preferred_element_type=jnp.float32)
    d_up = (d_hidden * pre_gate * sigmoid_gate).astype(jnp.bfloat16)
    d_gate = (d_hidden * pre_up * sigmoid_gate * (1.0 + pre_gate * (1.0 - sigmoid_gate))).astype(
        jnp.bfloat16
    )
    return (dot_cols(d_gate, token_keys), dot_cols(d_up, token_keys), dot_cols(d_output, hidden))


def renorm(weight, gradient):
    moved = weight - gradient
    keep = jnp.sqrt(jnp.sum(weight * weight, axis=1, keepdims=True))
    return moved * keep * lax.rsqrt(jnp.sum(moved * moved, axis=1, keepdims=True) + EPS_NORM)


def fast_apply(token_queries, gate_b, up_b, down_b):
    pre_gate = dot_rows(token_queries, gate_b)
    pre_up = dot_rows(token_queries, up_b)
    mixed = (pre_gate * jax.nn.sigmoid(pre_gate) * pre_up).astype(jnp.bfloat16)
    return dot_rows(mixed, down_b)


def normed_rows(fast_out, norm_gain):
    inverse = lax.rsqrt(jnp.mean(fast_out * fast_out, axis=1, keepdims=True) + EPS_NORM)
    return (fast_out * inverse * norm_gain[None, :]).astype(jnp.bfloat16)


def head_norm(projected, heads):
    count, features = projected.shape
    shaped = projected.reshape(count, heads, features // heads)
    shaped = shaped * lax.rsqrt(jnp.mean(shaped * shaped, axis=2, keepdims=True) + EPS_NORM)
    return shaped.reshape(count, features).astype(jnp.bfloat16)


def attend(q_rows, k_rows, v_rows, head_temper, half_span):
    heads = head_temper.shape[0]
    head_size = q_rows.shape[1] // heads
    query_count = q_rows.shape[0]
    key_count = k_rows.shape[0]
    offset = jnp.arange(key_count)[None, :] - half_span - jnp.arange(query_count)[:, None]
    inside = jnp.abs(offset) <= half_span

    def one_head(head):
        start = head * head_size
        query_h = lax.dynamic_slice_in_dim(q_rows, start, head_size, 1)
        key_h = lax.dynamic_slice_in_dim(k_rows, start, head_size, 1)
        value_h = lax.dynamic_slice_in_dim(v_rows, start, head_size, 1)
        scores = dot_rows(query_h, key_h) * (head_temper[head] / math.sqrt(head_size))
        scores = jnp.where(inside, scores, -1e30)
        highest = jnp.max(scores, axis=1, keepdims=True)
        weights = jnp.exp(scores - highest)
        weights = weights / jnp.sum(weights, axis=1, keepdims=True)
        return jnp.dot(weights.astype(jnp.bfloat16), value_h, preferred_element_type=jnp.float32)

    stacked = lax.map(one_head, jnp.arange(heads, dtype=jnp.int32))
    return jnp.transpose(stacked, (1, 0, 2)).reshape(query_count, heads * head_size)


def whole_matrices(mine, other, core):
    first = jnp.where(core == 0, mine, other)
    second = jnp.where(core == 0, other, mine)
    width = mine.shape[-1]
    return tuple(
        jnp.stack([first[:, m], second[:, m]], axis=1).reshape(-1, width) for m in range(3)
    )


def per_device(
    token_keys,
    token_values,
    token_queries,
    step_rates,
    fast_gate,
    fast_up,
    fast_down,
    norm_gain,
    proj_query,
    proj_key,
    proj_value,
    head_temper,
):
    row, col = lax.axis_index("row"), lax.axis_index("col")
    x, y = (row // 2) % NX, row // (2 * NX)
    z_hi, core = col // 2, col % 2
    width = token_keys.shape[1]
    shard = fast_gate.shape[0]
    piece = 3 * shard // 4

    core_swap = pairs(lambda x, y, z, c: (x, y, z, 1 - c))
    z_four = groups(lambda x, y, z, c: ((x, y, z % 2, c), z))
    z_eight = groups(lambda x, y, z, c: ((x, y, c), z))
    mixed_four = groups(
        lambda x, y, z, c: (("y", x, z, c), y) if c == 0 else (("x", y, z, c), x)
    )
    xy_sixteen = groups(lambda x, y, z, c: ((z, c), x * NY + y))

    owned = jnp.concatenate([fast_gate, fast_up, fast_down], axis=0)
    owned_b = owned.astype(jnp.bfloat16)
    part = jnp.where(core == 0, y, x)
    mine = lax.dynamic_slice_in_dim(owned_b, part * piece, piece, 0)
    quarter = exchange(spread(mine, 4).reshape(4 * piece, width), z_four)
    half = exchange(spread(quarter, 4).reshape(16 * piece, width), mixed_four)
    half = half.reshape(4, 4, piece, width).transpose(1, 0, 2, 3).reshape(4, 3, shard, width)
    other = lax.ppermute(half, ALL, core_swap)
    gate_all, up_all, down_all = whole_matrices(half, other, core)

    held = lax.dynamic_slice_in_dim(owned, y * piece, piece, 0)
    wide = jnp.where(z_hi == x, held, 0.0)
    for step in range(1, 4):
        sends = [
            (device_of(x, y, 2 * x + low, c), device_of(x, y, 2 * (x + step) + low, c))
            for x in range(NX)
            for y in range(NY)
            for low in range(2)
            for c in range(2)
        ]
        wide = wide + lax.ppermute(held, ALL, sends)

    grads = fast_gradients(token_keys, token_values, step_rates, gate_all, up_all, down_all)
    split = [g.reshape(4, 2, shard, width) for g in grads]
    keep = jnp.stack([lax.dynamic_index_in_dim(g, core, 1, False) for g in split], axis=1)
    give = jnp.stack(
        [lax.dynamic_index_in_dim(g, 1 - core, 1, False) for g in split], axis=1
    ).astype(jnp.bfloat16)
    taken = lax.ppermute(give, ALL, core_swap)
    chip_sum = (keep + taken.astype(jnp.float32)).astype(jnp.bfloat16)
    shares = exchange(chip_sum.reshape(16 * piece, width), xy_sixteen)
    plane = jnp.sum(shares.reshape(16, piece, width).astype(jnp.float32), axis=0)
    stack = exchange(
        spread(plane.astype(jnp.bfloat16), NZ).reshape(NZ * piece, width), z_eight
    )
    total = jnp.sum(stack.reshape(NZ, piece, width).astype(jnp.float32), axis=0)

    new_rows = renorm(wide, total).astype(jnp.bfloat16)
    half_new = exchange(spread(new_rows, 16).reshape(16 * piece, width), xy_sixteen)
    half_new = half_new.reshape(4, 3, shard, width)
    other_new = lax.ppermute(half_new, ALL, core_swap)
    gate_new_all, up_new_all, down_new_all = whole_matrices(half_new, other_new, core)
    own_new = lax.dynamic_index_in_dim(half_new, z_hi, 0, False).astype(jnp.float32)
    new_gate, new_up, new_down = own_new[0], own_new[1], own_new[2]

    fast_out = fast_apply(token_queries, gate_new_all, up_new_all, down_new_all)
    normed = normed_rows(fast_out, norm_gain)
    heads = head_temper.shape[0]
    query_n = head_norm(jnp.dot(normed, proj_query, preferred_element_type=jnp.float32), heads)
    key_n = head_norm(jnp.dot(normed, proj_key, preferred_element_type=jnp.float32), heads)
    value_b = jnp.dot(normed, proj_value, preferred_element_type=jnp.float32).astype(jnp.bfloat16)
    features = key_n.shape[1]
    half_span = token_keys.shape[0] // 2
    key_value = jnp.concatenate([key_n, value_b], axis=1)
    padded = padded_2(key_value, ((("row", "col"), 0),), half_span)
    attended = attend(query_n, padded[:, :features], padded[:, features:], head_temper, half_span)
    return (attended.astype(jnp.bfloat16), new_gate, new_up, new_down)


def solution(mesh):
    placed = (
        P(("row", "col"), None),
        P(("row", "col"), None),
        P(("row", "col"), None),
        P(("row", "col")),
        P("col", None),
        P("col", None),
        P("col", None),
        P(),
        P(),
        P(),
        P(),
        P(),
    )
    return jax.shard_map(
        per_device,
        mesh=mesh,
        in_specs=placed,
        out_specs=(P(("row", "col"), None), P("col", None), P("col", None), P("col", None)),
        check_vma=False,
    )
```

```python
import math

import jax
import jax.numpy as jnp
from jax import lax
from jax.experimental import pallas as pl
from jax.experimental.pallas import tpu as pltpu
from jax.sharding import PartitionSpec as P

EPS_NORM = 1e-06
NX, NY, NZ = 4, 4, 8
ALL = ("row", "col")


def device_of(x, y, z, c):
    x, y, z = x % NX, y % NY, z % NZ
    return ((y * NX + x) * 2 + z % 2) * 8 + (z // 2) * 2 + c


def places():
    return [
        (x, y, z, c) for x in range(NX) for y in range(NY) for z in range(NZ) for c in range(2)
    ]


def pairs(target):
    return [(device_of(*p), device_of(*target(*p))) for p in places()]


def groups(key):
    found = {}
    for p in places():
        name, order = key(*p)
        found.setdefault(name, []).append((order, device_of(*p)))
    return [[device for _, device in sorted(members)] for members in found.values()]


def exchange(blocks, group):
    return lax.all_to_all(blocks, ALL, 0, 0, axis_index_groups=group, tiled=True)


def spread(block, count):
    return jnp.broadcast_to(block[None], (count,) + block.shape)


def dot_rows(left, right):
    return lax.dot_general(
        left, right, (((1,), (1,)), ((), ())), preferred_element_type=jnp.float32
    )


def dot_cols(left, right):
    return lax.dot_general(
        left, right, (((0,), (0,)), ((), ())), preferred_element_type=jnp.float32
    )


def fast_gradients(token_keys, token_values, step_rates, gate_b, up_b, down_b):
    pre_gate = dot_rows(token_keys, gate_b)
    pre_up = dot_rows(token_keys, up_b)
    sigmoid_gate = jax.nn.sigmoid(pre_gate)
    hidden = (pre_gate * sigmoid_gate * pre_up).astype(jnp.bfloat16)
    d_output = (-step_rates[:, None] * token_values.astype(jnp.float32)).astype(jnp.bfloat16)
    d_hidden = jnp.dot(d_output, down_b, preferred_element_type=jnp.float32)
    d_up = (d_hidden * pre_gate * sigmoid_gate).astype(jnp.bfloat16)
    d_gate = (d_hidden * pre_up * sigmoid_gate * (1.0 + pre_gate * (1.0 - sigmoid_gate))).astype(
        jnp.bfloat16
    )
    return (dot_cols(d_gate, token_keys), dot_cols(d_up, token_keys), dot_cols(d_output, hidden))


def renorm(weight, gradient):
    moved = weight - gradient
    keep = jnp.sqrt(jnp.sum(weight * weight, axis=1, keepdims=True))
    return moved * keep * lax.rsqrt(jnp.sum(moved * moved, axis=1, keepdims=True) + EPS_NORM)


def project_kernel(
    core_ref,
    x_ref,
    mine_ref,
    other_ref,
    gain_ref,
    query_ref,
    key_ref,
    value_ref,
    fold_ref,
    unfold_ref,
    q_ref,
    k_ref,
    v_ref,
    whole,
    sems,
):
    step = pl.program_id(0)
    core = core_ref[0]
    bands, _, rows, _ = mine_ref.shape

    def copies():
        found = []
        for m in range(3):
            for band in range(bands):
                for i, (source, seat) in enumerate(((mine_ref, core), (other_ref, 1 - core))):
                    start = pl.multiple_of(band * 2 * rows + seat * rows, rows)
                    found.append(
                        pltpu.make_async_copy(
                            source.at[band, m],
                            whole.at[m, pl.ds(start, rows)],
                            sems.at[m, band, i],
                        )
                    )
        return found

    @pl.when(step == 0)
    def _():
        for copy in copies():
            copy.start()
        for copy in copies():
            copy.wait()

    tokens = x_ref[...]
    pre_gate = dot_rows(tokens, whole[0])
    pre_up = dot_rows(tokens, whole[1])
    mixed = (pre_gate * jax.nn.sigmoid(pre_gate) * pre_up).astype(jnp.bfloat16)
    fast_out = dot_rows(mixed, whole[2])
    inverse = lax.rsqrt(jnp.mean(fast_out * fast_out, axis=1, keepdims=True) + EPS_NORM)
    normed = (fast_out * inverse * gain_ref[...]).astype(jnp.bfloat16)

    def head_norm(matrix_ref):
        projected = jnp.dot(normed, matrix_ref[...], preferred_element_type=jnp.float32)
        square = jnp.dot(
            projected * projected,
            fold_ref[...],
            precision=lax.Precision.HIGHEST,
            preferred_element_type=jnp.float32,
        )
        scale = jnp.dot(
            lax.rsqrt(square + EPS_NORM),
            unfold_ref[...],
            precision=lax.Precision.HIGHEST,
            preferred_element_type=jnp.float32,
        )
        return (projected * scale).astype(jnp.bfloat16)

    k_ref[...] = head_norm(key_ref)
    v_ref[...] = jnp.dot(normed, value_ref[...], preferred_element_type=jnp.float32).astype(
        jnp.bfloat16
    )

    @pl.when((step >= 1) & (step < pl.num_programs(0) - 1))
    def _():
        q_ref[...] = head_norm(query_ref)


def project(core, tokens, mine, other, norm_gain, proj_query, proj_key, proj_value, heads):
    count, width = tokens.shape
    block = count // 4
    lane = jnp.arange(width)[:, None] // (width // heads) == jnp.arange(128)[None, :]
    fold = lane.astype(jnp.float32) * (heads / width)
    unfold = lane.T.astype(jnp.float32)
    fixed = lambda *shape: pl.BlockSpec(shape, lambda i, c: (0,) * len(shape))
    anywhere = pl.BlockSpec(memory_space=pl.ANY)
    rows = pl.BlockSpec((block, width), lambda i, c: (i, 0))
    flops = 2 * count * width * width * 5 + count * width * width
    return pl.pallas_call(
        project_kernel,
        grid_spec=pltpu.PrefetchScalarGridSpec(
            num_scalar_prefetch=1,
            grid=(4,),
            in_specs=[
                rows,
                anywhere,
                anywhere,
                fixed(1, width),
                fixed(width, width),
                fixed(width, width),
                fixed(width, width),
                fixed(width, 128),
                fixed(128, width),
            ],
            out_specs=[
                pl.BlockSpec((block, width), lambda i, c: (jnp.clip(i - 1, 0, 1), 0)),
                rows,
                rows,
            ],
            scratch_shapes=[
                pltpu.VMEM((3, width, width), jnp.bfloat16),
                pltpu.SemaphoreType.DMA((3, mine.shape[0], 2)),
            ],
        ),
        out_shape=[
            jax.ShapeDtypeStruct((count // 2, width), jnp.bfloat16),
            jax.ShapeDtypeStruct((count, width), jnp.bfloat16),
            jax.ShapeDtypeStruct((count, width), jnp.bfloat16),
        ],
        cost_estimate=pl.CostEstimate(
            flops=flops, bytes_accessed=12 * width * width + 8 * count * width, transcendentals=0
        ),
        name="project",
    )(
        core.reshape(1),
        tokens,
        mine,
        other,
        norm_gain.reshape(1, width),
        proj_query,
        proj_key,
        proj_value,
        fold,
        unfold,
    )


def attend_kernel(span, temper_ref, q_ref, k_ref, v_ref, o_ref):
    pair = pl.program_id(0)
    lanes = q_ref.shape[1]
    size = lanes // 2
    block = 128
    keys = block + 2 * span
    lane = lax.broadcasted_iota(jnp.int32, (block, lanes), 1)
    ahead = lax.broadcasted_iota(jnp.int32, (block, block), 1) - lax.broadcasted_iota(
        jnp.int32, (block, block), 0
    )
    for start in range(0, q_ref.shape[0], block):
        q_rows = q_ref[start : start + block, :]
        k_rows = k_ref[start : start + keys, :]
        v_rows = v_ref[start : start + keys, :]
        results = []
        for head in range(2):
            inside = (lane < size) if head == 0 else (lane >= size)
            scale = temper_ref[2 * pair + head] * (1.0 / math.sqrt(size) / math.log(2.0))
            scores = dot_rows(jnp.where(inside, q_rows, jnp.zeros_like(q_rows)), k_rows)
            scores = jnp.concatenate(
                [
                    jnp.where(ahead >= 0, scores[:, :block], -1e30),
                    scores[:, block : keys - block],
                    jnp.where(ahead <= 0, scores[:, keys - block :], -1e30),
                ],
                axis=1,
            )
            highest = jnp.max(scores, axis=1, keepdims=True)
            weights = jnp.exp2((scores - highest) * scale)
            total = jnp.sum(weights, axis=1, keepdims=True)
            mixed = jnp.dot(
                weights.astype(jnp.bfloat16), v_rows, preferred_element_type=jnp.float32
            )
            results.append(mixed / total)
        o_ref[start : start + block, :] = jnp.where(
            lane < size, results[0], results[1]
        ).astype(jnp.bfloat16)


def attend(q_rows, k_rows, v_rows, head_temper):
    count, width = q_rows.shape
    span = (k_rows.shape[0] - count) // 2
    heads = head_temper.shape[0]
    lanes = 2 * width // heads
    wide = lambda size: pl.BlockSpec((size, lanes), lambda h, t: (0, h))
    return pl.pallas_call(
        lambda *refs: attend_kernel(span, *refs),
        grid_spec=pltpu.PrefetchScalarGridSpec(
            num_scalar_prefetch=1,
            grid=(heads // 2,),
            in_specs=[wide(count), wide(count + 2 * span), wide(count + 2 * span)],
            out_specs=wide(count),
        ),
        out_shape=jax.ShapeDtypeStruct((count, width), jnp.bfloat16),
        cost_estimate=pl.CostEstimate(
            flops=4 * count * (2 * span + 128) * width,
            bytes_accessed=16 * count * width,
            transcendentals=count * heads * (2 * span + 128),
        ),
        name="attend",
    )(head_temper, q_rows, k_rows, v_rows)


def whole_matrices(mine, other, core):
    first = jnp.where(core == 0, mine, other)
    second = jnp.where(core == 0, other, mine)
    width = mine.shape[-1]
    return tuple(
        jnp.stack([first[:, m], second[:, m]], axis=1).reshape(-1, width) for m in range(3)
    )


def per_device(
    token_keys,
    token_values,
    token_queries,
    step_rates,
    fast_gate,
    fast_up,
    fast_down,
    norm_gain,
    proj_query,
    proj_key,
    proj_value,
    head_temper,
):
    row, col = lax.axis_index("row"), lax.axis_index("col")
    x, y = (row // 2) % NX, row // (2 * NX)
    z_hi, core = col // 2, col % 2
    width = token_keys.shape[1]
    shard = fast_gate.shape[0]
    piece = 3 * shard // 4

    core_swap = pairs(lambda x, y, z, c: (x, y, z, 1 - c))
    z_four = groups(lambda x, y, z, c: ((x, y, z % 2, c), z))
    z_eight = groups(lambda x, y, z, c: ((x, y, c), z))
    mixed_four = groups(
        lambda x, y, z, c: (("y", x, z, c), y) if c == 0 else (("x", y, z, c), x)
    )
    xy_sixteen = groups(lambda x, y, z, c: ((z, c), x * NY + y))

    owned = jnp.concatenate([fast_gate, fast_up, fast_down], axis=0)
    owned_b = owned.astype(jnp.bfloat16)
    part = jnp.where(core == 0, y, x)
    mine = lax.dynamic_slice_in_dim(owned_b, part * piece, piece, 0)
    quarter = exchange(spread(mine, 4).reshape(4 * piece, width), z_four)
    half = exchange(spread(quarter, 4).reshape(16 * piece, width), mixed_four)
    half = half.reshape(4, 4, piece, width).transpose(1, 0, 2, 3).reshape(4, 3, shard, width)
    other = lax.ppermute(half, ALL, core_swap)
    gate_all, up_all, down_all = whole_matrices(half, other, core)

    held = lax.dynamic_slice_in_dim(owned, y * piece, piece, 0)
    wide = jnp.where(z_hi == x, held, 0.0)
    for step in range(1, 4):
        sends = [
            (device_of(x, y, 2 * x + low, c), device_of(x, y, 2 * (x + step) + low, c))
            for x in range(NX)
            for y in range(NY)
            for low in range(2)
            for c in range(2)
        ]
        wide = wide + lax.ppermute(held, ALL, sends)

    count = lax.axis_size("row") * lax.axis_size("col")
    span = token_queries.shape[0] // 2
    tokens = jnp.concatenate(
        [
            lax.ppermute(token_queries[span:], ALL, [(i, (i + 1) % count) for i in range(count)]),
            token_queries,
            lax.ppermute(token_queries[:span], ALL, [((i + 1) % count, i) for i in range(count)]),
        ],
        axis=0,
    )

    grads = fast_gradients(token_keys, token_values, step_rates, gate_all, up_all, down_all)
    split = [g.reshape(4, 2, shard, width) for g in grads]
    keep = jnp.stack([lax.dynamic_index_in_dim(g, core, 1, False) for g in split], axis=1)
    give = jnp.stack(
        [lax.dynamic_index_in_dim(g, 1 - core, 1, False) for g in split], axis=1
    ).astype(jnp.bfloat16)
    taken = lax.ppermute(give, ALL, core_swap)
    chip_sum = (keep + taken.astype(jnp.float32)).astype(jnp.bfloat16)
    shares = exchange(chip_sum.reshape(16 * piece, width), xy_sixteen)
    plane = jnp.sum(shares.reshape(16, piece, width).astype(jnp.float32), axis=0)
    stack = exchange(
        spread(plane.astype(jnp.bfloat16), NZ).reshape(NZ * piece, width), z_eight
    )
    total = jnp.sum(stack.reshape(NZ, piece, width).astype(jnp.float32), axis=0)

    new_rows = renorm(wide, total).astype(jnp.bfloat16)
    half_new = exchange(spread(new_rows, 16).reshape(16 * piece, width), xy_sixteen)
    half_new = half_new.reshape(4, 3, shard, width)
    other_new = lax.ppermute(half_new, ALL, core_swap)
    own_new = lax.dynamic_index_in_dim(half_new, z_hi, 0, False).astype(jnp.float32)
    new_gate, new_up, new_down = own_new[0], own_new[1], own_new[2]

    heads = head_temper.shape[0]
    query_n, key_n, value_b = project(
        core, tokens, half_new, other_new, norm_gain, proj_query, proj_key, proj_value, heads
    )
    attended = attend(query_n, key_n, value_b, head_temper)
    return (attended, new_gate, new_up, new_down)


def solution(mesh):
    placed = (
        P(("row", "col"), None),
        P(("row", "col"), None),
        P(("row", "col"), None),
        P(("row", "col")),
        P("col", None),
        P("col", None),
        P("col", None),
        P(),
        P(),
        P(),
        P(),
        P(),
    )
    return jax.shard_map(
        per_device,
        mesh=mesh,
        in_specs=placed,
        out_specs=(P(("row", "col"), None), P("col", None), P("col", None), P("col", None)),
        check_vma=False,
    )
```

```python
import math

import jax
import jax.numpy as jnp
from jax import lax
from jax.experimental import pallas as pl
from jax.experimental.pallas import tpu as pltpu
from jax.sharding import PartitionSpec as P

EPS_NORM = 1e-06
NX, NY, NZ = 4, 4, 8
ALL = ("row", "col")


def device_of(x, y, z, c):
    x, y, z = x % NX, y % NY, z % NZ
    return ((y * NX + x) * 2 + z % 2) * 8 + (z // 2) * 2 + c


def places():
    return [
        (x, y, z, c) for x in range(NX) for y in range(NY) for z in range(NZ) for c in range(2)
    ]


def pairs(target):
    return [(device_of(*p), device_of(*target(*p))) for p in places()]


def groups(key):
    found = {}
    for p in places():
        name, order = key(*p)
        found.setdefault(name, []).append((order, device_of(*p)))
    return [[device for _, device in sorted(members)] for members in found.values()]


def exchange(blocks, group):
    return lax.all_to_all(blocks, ALL, 0, 0, axis_index_groups=group, tiled=True)


def spread(block, count):
    return jnp.broadcast_to(block[None], (count,) + block.shape)


def dot_rows(left, right):
    return lax.dot_general(
        left, right, (((1,), (1,)), ((), ())), preferred_element_type=jnp.float32
    )


def dot_cols(left, right):
    return lax.dot_general(
        left, right, (((0,), (0,)), ((), ())), preferred_element_type=jnp.float32
    )


def dot_split(left, right):
    high = left.astype(jnp.bfloat16)
    low = (left - high.astype(jnp.float32)).astype(jnp.bfloat16)
    return jnp.dot(high, right, preferred_element_type=jnp.float32) + jnp.dot(
        low, right, preferred_element_type=jnp.float32
    )


def whole_copies(core, mine_ref, other_ref, whole, sems):
    bands, _, rows, _ = mine_ref.shape
    found = []
    for m in range(3):
        for band in range(bands):
            for i, (source, seat) in enumerate(((mine_ref, core), (other_ref, 1 - core))):
                start = pl.multiple_of(band * 2 * rows + seat * rows, rows)
                found.append(
                    pltpu.make_async_copy(
                        source.at[band, m], whole.at[m, pl.ds(start, rows)], sems.at[m, band, i]
                    )
                )
    return found


def gradient_kernel(
    core_ref,
    keys_ref,
    values_ref,
    rates_ref,
    mine_ref,
    other_ref,
    keep_ref,
    give_ref,
    whole,
    d_output,
    rows_sum,
    down_sum,
    sems,
):
    step = pl.program_id(0)
    core = core_ref[0]
    bands, _, rows, _ = mine_ref.shape
    chunk = rows_sum.shape[0]
    half_bands = chunk // (2 * rows)

    @pl.when(step == 0)
    def _():
        for copy in whole_copies(core, mine_ref, other_ref, whole, sems):
            copy.start()
        d_output[...] = (-rates_ref[...] * values_ref[...].astype(jnp.float32)).astype(
            jnp.bfloat16
        )
        for copy in whole_copies(core, mine_ref, other_ref, whole, sems):
            copy.wait()

    tokens = keys_ref[...]
    start = pl.multiple_of(step * chunk, chunk)
    pre_gate = dot_rows(tokens, whole[0, pl.ds(start, chunk), :])
    pre_up = dot_rows(tokens, whole[1, pl.ds(start, chunk), :])
    sig = jax.nn.sigmoid(pre_gate)
    hidden = (pre_gate * sig * pre_up).astype(jnp.bfloat16)
    d_hidden = jnp.dot(
        d_output[...], whole[2, :, pl.ds(start, chunk)], preferred_element_type=jnp.float32
    )
    d_up = (d_hidden * pre_gate * sig).astype(jnp.bfloat16)
    d_gate = (d_hidden * pre_up * sig * (1.0 + pre_gate * (1.0 - sig))).astype(jnp.bfloat16)
    down_sum[:, pl.ds(start, chunk)] = dot_cols(d_output[...], hidden)

    def put(m, band, source, at):
        mine_at = pl.multiple_of(at + core * rows, rows)
        other_at = pl.multiple_of(at + (1 - core) * rows, rows)
        keep_ref[band, m] = source[pl.ds(mine_at, rows), :].astype(jnp.bfloat16)
        give_ref[band, m] = source[pl.ds(other_at, rows), :].astype(jnp.bfloat16)

    for m, slope in ((0, d_gate), (1, d_up)):
        rows_sum[...] = dot_cols(slope, tokens)
        for i in range(half_bands):
            put(m, step * half_bands + i, rows_sum, i * 2 * rows)

    @pl.when(step == pl.num_programs(0) - 1)
    def _():
        for band in range(bands):
            put(2, band, down_sum, band * 2 * rows)


def gradients(core, token_keys, token_values, step_rates, mine, other):
    count, width = token_keys.shape
    shape = mine.shape
    chunk = width // 2
    fixed = lambda *size: pl.BlockSpec(size, lambda i, c: (0,) * len(size))
    anywhere = pl.BlockSpec(memory_space=pl.ANY)
    return pl.pallas_call(
        gradient_kernel,
        grid_spec=pltpu.PrefetchScalarGridSpec(
            num_scalar_prefetch=1,
            grid=(2,),
            in_specs=[
                fixed(count, width),
                fixed(count, width),
                fixed(count, 1),
                anywhere,
                anywhere,
            ],
            out_specs=[fixed(*shape), fixed(*shape)],
            scratch_shapes=[
                pltpu.VMEM((3, width, width), jnp.bfloat16),
                pltpu.VMEM((count, width), jnp.bfloat16),
                pltpu.VMEM((chunk, width), jnp.float32),
                pltpu.VMEM((width, width), jnp.float32),
                pltpu.SemaphoreType.DMA((3, shape[0], 2)),
            ],
        ),
        out_shape=[jax.ShapeDtypeStruct(shape, jnp.bfloat16)] * 2,
        cost_estimate=pl.CostEstimate(
            flops=12 * count * width * width,
            bytes_accessed=4 * count * width + 12 * width * width,
            transcendentals=count * width,
        ),
        name="gradients",
    )(core.reshape(1), token_keys, token_values, step_rates.reshape(count, 1), mine, other)


def renorm(weight, gradient):
    moved = weight - gradient
    keep = jnp.sqrt(jnp.sum(weight * weight, axis=1, keepdims=True))
    return moved * keep * lax.rsqrt(jnp.sum(moved * moved, axis=1, keepdims=True) + EPS_NORM)


def project_kernel(
    core_ref,
    x_ref,
    mine_ref,
    other_ref,
    gain_ref,
    query_ref,
    key_ref,
    value_ref,
    fold_ref,
    unfold_ref,
    q_ref,
    k_ref,
    v_ref,
    whole,
    sems,
):
    step = pl.program_id(0)
    core = core_ref[0]

    @pl.when(step == 0)
    def _():
        for copy in whole_copies(core, mine_ref, other_ref, whole, sems):
            copy.start()
        for copy in whole_copies(core, mine_ref, other_ref, whole, sems):
            copy.wait()

    tokens = x_ref[...]
    pre_gate = dot_rows(tokens, whole[0])
    pre_up = dot_rows(tokens, whole[1])
    mixed = (pre_gate * jax.nn.sigmoid(pre_gate) * pre_up).astype(jnp.bfloat16)
    fast_out = dot_rows(mixed, whole[2])
    inverse = lax.rsqrt(jnp.mean(fast_out * fast_out, axis=1, keepdims=True) + EPS_NORM)
    normed = (fast_out * inverse * gain_ref[...]).astype(jnp.bfloat16)

    def head_norm(matrix_ref):
        projected = jnp.dot(normed, matrix_ref[...], preferred_element_type=jnp.float32)
        square = dot_split(projected * projected, fold_ref[...])
        scale = dot_split(lax.rsqrt(square + EPS_NORM), unfold_ref[...])
        return (projected * scale).astype(jnp.bfloat16)

    k_ref[...] = head_norm(key_ref)
    v_ref[...] = jnp.dot(normed, value_ref[...], preferred_element_type=jnp.float32).astype(
        jnp.bfloat16
    )

    @pl.when((step >= 1) & (step < pl.num_programs(0) - 1))
    def _():
        q_ref[...] = head_norm(query_ref)


def project(core, tokens, mine, other, norm_gain, proj_query, proj_key, proj_value, heads):
    count, width = tokens.shape
    block = count // 4
    lane = jnp.arange(width)[:, None] // (width // heads) == jnp.arange(128)[None, :]
    fold = (lane * (heads / width)).astype(jnp.bfloat16)
    unfold = lane.T.astype(jnp.bfloat16)
    fixed = lambda *shape: pl.BlockSpec(shape, lambda i, c: (0,) * len(shape))
    anywhere = pl.BlockSpec(memory_space=pl.ANY)
    rows = pl.BlockSpec((block, width), lambda i, c: (i, 0))
    flops = 2 * count * width * width * 5 + count * width * width
    return pl.pallas_call(
        project_kernel,
        grid_spec=pltpu.PrefetchScalarGridSpec(
            num_scalar_prefetch=1,
            grid=(4,),
            in_specs=[
                rows,
                anywhere,
                anywhere,
                fixed(1, width),
                fixed(width, width),
                fixed(width, width),
                fixed(width, width),
                fixed(width, 128),
                fixed(128, width),
            ],
            out_specs=[
                pl.BlockSpec((block, width), lambda i, c: (jnp.clip(i - 1, 0, 1), 0)),
                rows,
                rows,
            ],
            scratch_shapes=[
                pltpu.VMEM((3, width, width), jnp.bfloat16),
                pltpu.SemaphoreType.DMA((3, mine.shape[0], 2)),
            ],
        ),
        out_shape=[
            jax.ShapeDtypeStruct((count // 2, width), jnp.bfloat16),
            jax.ShapeDtypeStruct((count, width), jnp.bfloat16),
            jax.ShapeDtypeStruct((count, width), jnp.bfloat16),
        ],
        cost_estimate=pl.CostEstimate(
            flops=flops, bytes_accessed=12 * width * width + 8 * count * width, transcendentals=0
        ),
        name="project",
    )(
        core.reshape(1),
        tokens,
        mine,
        other,
        norm_gain.reshape(1, width),
        proj_query,
        proj_key,
        proj_value,
        fold,
        unfold,
    )


def attend_kernel(span, temper_ref, q_ref, k_ref, v_ref, o_ref):
    pair = pl.program_id(0)
    lanes = q_ref.shape[1]
    size = lanes // 2
    block = 128
    keys = block + 2 * span
    lane = lax.broadcasted_iota(jnp.int32, (block, lanes), 1)
    ahead = lax.broadcasted_iota(jnp.int32, (block, block), 1) - lax.broadcasted_iota(
        jnp.int32, (block, block), 0
    )
    for start in range(0, q_ref.shape[0], block):
        q_rows = q_ref[start : start + block, :]
        k_rows = k_ref[start : start + keys, :]
        v_rows = v_ref[start : start + keys, :]
        results = []
        for head in range(2):
            inside = (lane < size) if head == 0 else (lane >= size)
            scale = temper_ref[2 * pair + head] * (1.0 / math.sqrt(size) / math.log(2.0))
            scores = dot_rows(jnp.where(inside, q_rows, jnp.zeros_like(q_rows)), k_rows)
            scores = jnp.concatenate(
                [
                    jnp.where(ahead >= 0, scores[:, :block], -1e30),
                    scores[:, block : keys - block],
                    jnp.where(ahead <= 0, scores[:, keys - block :], -1e30),
                ],
                axis=1,
            )
            highest = jnp.max(scores, axis=1, keepdims=True)
            weights = jnp.exp2((scores - highest) * scale)
            total = jnp.sum(weights, axis=1, keepdims=True)
            mixed = jnp.dot(
                weights.astype(jnp.bfloat16), v_rows, preferred_element_type=jnp.float32
            )
            results.append(mixed / total)
        o_ref[start : start + block, :] = jnp.where(
            lane < size, results[0], results[1]
        ).astype(jnp.bfloat16)


def attend(q_rows, k_rows, v_rows, head_temper):
    count, width = q_rows.shape
    span = (k_rows.shape[0] - count) // 2
    heads = head_temper.shape[0]
    lanes = 2 * width // heads
    wide = lambda size: pl.BlockSpec((size, lanes), lambda h, t: (0, h))
    return pl.pallas_call(
        lambda *refs: attend_kernel(span, *refs),
        grid_spec=pltpu.PrefetchScalarGridSpec(
            num_scalar_prefetch=1,
            grid=(heads // 2,),
            in_specs=[wide(count), wide(count + 2 * span), wide(count + 2 * span)],
            out_specs=wide(count),
        ),
        out_shape=jax.ShapeDtypeStruct((count, width), jnp.bfloat16),
        cost_estimate=pl.CostEstimate(
            flops=4 * count * (2 * span + 128) * width,
            bytes_accessed=16 * count * width,
            transcendentals=count * heads * (2 * span + 128),
        ),
        name="attend",
    )(head_temper, q_rows, k_rows, v_rows)


def per_device(
    token_keys,
    token_values,
    token_queries,
    step_rates,
    fast_gate,
    fast_up,
    fast_down,
    norm_gain,
    proj_query,
    proj_key,
    proj_value,
    head_temper,
):
    row, col = lax.axis_index("row"), lax.axis_index("col")
    x, y = (row // 2) % NX, row // (2 * NX)
    z_hi, core = col // 2, col % 2
    width = token_keys.shape[1]
    shard = fast_gate.shape[0]
    piece = 3 * shard // 4

    core_swap = pairs(lambda x, y, z, c: (x, y, z, 1 - c))
    z_four = groups(lambda x, y, z, c: ((x, y, z % 2, c), z))
    z_eight = groups(lambda x, y, z, c: ((x, y, c), z))
    mixed_four = groups(
        lambda x, y, z, c: (("y", x, z, c), y) if c == 0 else (("x", y, z, c), x)
    )
    xy_sixteen = groups(lambda x, y, z, c: ((z, c), x * NY + y))

    owned = jnp.concatenate([fast_gate, fast_up, fast_down], axis=0)
    owned_b = owned.astype(jnp.bfloat16)
    part = jnp.where(core == 0, y, x)
    mine = lax.dynamic_slice_in_dim(owned_b, part * piece, piece, 0)
    quarter = exchange(spread(mine, 4).reshape(4 * piece, width), z_four)
    half = exchange(spread(quarter, 4).reshape(16 * piece, width), mixed_four)
    half = half.reshape(4, 4, piece, width).transpose(1, 0, 2, 3).reshape(4, 3, shard, width)
    other = lax.ppermute(half, ALL, core_swap)
    other, held, queries = lax.optimization_barrier((other, owned, token_queries))

    held = lax.dynamic_slice_in_dim(held, y * piece, piece, 0)
    wide = jnp.where(z_hi == x, held, 0.0)
    for step in range(1, 4):
        sends = [
            (device_of(x, y, 2 * x + low, c), device_of(x, y, 2 * (x + step) + low, c))
            for x in range(NX)
            for y in range(NY)
            for low in range(2)
            for c in range(2)
        ]
        wide = wide + lax.ppermute(held, ALL, sends)

    count = lax.axis_size("row") * lax.axis_size("col")
    span = token_queries.shape[0] // 2
    before = lax.ppermute(queries[span:], ALL, [(i, (i + 1) % count) for i in range(count)])
    after = lax.ppermute(queries[:span], ALL, [((i + 1) % count, i) for i in range(count)])

    keep, give = gradients(core, token_keys, token_values, step_rates, half, other)
    give, before, after, wide = lax.optimization_barrier((give, before, after, wide))
    tokens = jnp.concatenate([before, token_queries, after], axis=0)
    taken = lax.ppermute(give, ALL, core_swap)
    chip_sum = (keep.astype(jnp.float32) + taken.astype(jnp.float32)).astype(jnp.bfloat16)
    shares = exchange(chip_sum.reshape(16 * piece, width), xy_sixteen)
    plane = jnp.sum(shares.reshape(16, piece, width).astype(jnp.float32), axis=0)
    stack = exchange(
        spread(plane.astype(jnp.bfloat16), NZ).reshape(NZ * piece, width), z_eight
    )
    total = jnp.sum(stack.reshape(NZ, piece, width).astype(jnp.float32), axis=0)

    new_rows = renorm(wide, total).astype(jnp.bfloat16)
    half_new = exchange(spread(new_rows, 16).reshape(16 * piece, width), xy_sixteen)
    half_new = half_new.reshape(4, 3, shard, width)
    other_new = lax.ppermute(half_new, ALL, core_swap)
    own_new = lax.dynamic_index_in_dim(half_new, z_hi, 0, False).astype(jnp.float32)
    new_gate, new_up, new_down = own_new[0], own_new[1], own_new[2]

    heads = head_temper.shape[0]
    query_n, key_n, value_b = project(
        core, tokens, half_new, other_new, norm_gain, proj_query, proj_key, proj_value, heads
    )
    attended = attend(query_n, key_n, value_b, head_temper)
    return (attended, new_gate, new_up, new_down)


def solution(mesh):
    placed = (
        P(("row", "col"), None),
        P(("row", "col"), None),
        P(("row", "col"), None),
        P(("row", "col")),
        P("col", None),
        P("col", None),
        P("col", None),
        P(),
        P(),
        P(),
        P(),
        P(),
    )
    return jax.shard_map(
        per_device,
        mesh=mesh,
        in_specs=placed,
        out_specs=(P(("row", "col"), None), P("col", None), P("col", None), P("col", None)),
        check_vma=False,
    )
```

```python
import math

import jax
import jax.numpy as jnp
from jax import lax
from jax.experimental import pallas as pl
from jax.experimental.pallas import tpu as pltpu
from jax.sharding import PartitionSpec as P

EPS_NORM = 1e-06
NX, NY, NZ = 4, 4, 8
ALL = ("row", "col")


def device_of(x, y, z, c):
    x, y, z = x % NX, y % NY, z % NZ
    return ((y * NX + x) * 2 + z % 2) * 8 + (z // 2) * 2 + c


def places():
    return [
        (x, y, z, c) for x in range(NX) for y in range(NY) for z in range(NZ) for c in range(2)
    ]


def pairs(target):
    return [(device_of(*p), device_of(*target(*p))) for p in places()]


def groups(key):
    found = {}
    for p in places():
        name, order = key(*p)
        found.setdefault(name, []).append((order, device_of(*p)))
    return [[device for _, device in sorted(members)] for members in found.values()]


def exchange(blocks, group):
    return lax.all_to_all(blocks, ALL, 0, 0, axis_index_groups=group, tiled=True)


def spread(block, count):
    return jnp.broadcast_to(block[None], (count,) + block.shape)


def dot_rows(left, right):
    return lax.dot_general(
        left, right, (((1,), (1,)), ((), ())), preferred_element_type=jnp.float32
    )


def dot_cols(left, right):
    return lax.dot_general(
        left, right, (((0,), (0,)), ((), ())), preferred_element_type=jnp.float32
    )


def dot_split(left, right):
    high = left.astype(jnp.bfloat16)
    low = (left - high.astype(jnp.float32)).astype(jnp.bfloat16)
    return jnp.dot(high, right, preferred_element_type=jnp.float32) + jnp.dot(
        low, right, preferred_element_type=jnp.float32
    )


def whole_copies(core, mine_ref, other_ref, whole, sems):
    bands, _, rows, _ = mine_ref.shape
    found = []
    for m in range(3):
        for band in range(bands):
            for i, (source, seat) in enumerate(((mine_ref, core), (other_ref, 1 - core))):
                start = pl.multiple_of(band * 2 * rows + seat * rows, rows)
                found.append(
                    pltpu.make_async_copy(
                        source.at[band, m], whole.at[m, pl.ds(start, rows)], sems.at[m, band, i]
                    )
                )
    return found


def gradient_kernel(
    core_ref,
    keys_ref,
    values_ref,
    rates_ref,
    mine_ref,
    other_ref,
    keep_ref,
    give_ref,
    whole,
    d_output,
    rows_sum,
    down_sum,
    sems,
):
    step = pl.program_id(0)
    core = core_ref[0]
    bands, _, rows, _ = mine_ref.shape
    chunk = rows_sum.shape[0]
    half_bands = chunk // (2 * rows)

    @pl.when(step == 0)
    def _():
        for copy in whole_copies(core, mine_ref, other_ref, whole, sems):
            copy.start()
        d_output[...] = (-rates_ref[...] * values_ref[...].astype(jnp.float32)).astype(
            jnp.bfloat16
        )
        for copy in whole_copies(core, mine_ref, other_ref, whole, sems):
            copy.wait()

    tokens = keys_ref[...]
    start = pl.multiple_of(step * chunk, chunk)
    pre_gate = dot_rows(tokens, whole[0, pl.ds(start, chunk), :])
    pre_up = dot_rows(tokens, whole[1, pl.ds(start, chunk), :])
    sig = jax.nn.sigmoid(pre_gate)
    hidden = (pre_gate * sig * pre_up).astype(jnp.bfloat16)
    d_hidden = jnp.dot(
        d_output[...], whole[2, :, pl.ds(start, chunk)], preferred_element_type=jnp.float32
    )
    d_up = (d_hidden * pre_gate * sig).astype(jnp.bfloat16)
    d_gate = (d_hidden * pre_up * sig * (1.0 + pre_gate * (1.0 - sig))).astype(jnp.bfloat16)
    down_sum[:, pl.ds(start, chunk)] = dot_cols(d_output[...], hidden)

    def put(m, band, source, at):
        mine_at = pl.multiple_of(at + core * rows, rows)
        other_at = pl.multiple_of(at + (1 - core) * rows, rows)
        keep_ref[band, m] = source[pl.ds(mine_at, rows), :].astype(jnp.bfloat16)
        give_ref[band, m] = source[pl.ds(other_at, rows), :].astype(jnp.bfloat16)

    for m, slope in ((0, d_gate), (1, d_up)):
        rows_sum[...] = dot_cols(slope, tokens)
        for i in range(half_bands):
            put(m, step * half_bands + i, rows_sum, i * 2 * rows)

    @pl.when(step == pl.num_programs(0) - 1)
    def _():
        for band in range(bands):
            put(2, band, down_sum, band * 2 * rows)


def gradients(core, token_keys, token_values, step_rates, mine, other):
    count, width = token_keys.shape
    shape = mine.shape
    chunk = width // 2
    fixed = lambda *size: pl.BlockSpec(size, lambda i, c: (0,) * len(size))
    anywhere = pl.BlockSpec(memory_space=pl.ANY)
    return pl.pallas_call(
        gradient_kernel,
        grid_spec=pltpu.PrefetchScalarGridSpec(
            num_scalar_prefetch=1,
            grid=(2,),
            in_specs=[
                fixed(count, width),
                fixed(count, width),
                fixed(count, 1),
                anywhere,
                anywhere,
            ],
            out_specs=[fixed(*shape), fixed(*shape)],
            scratch_shapes=[
                pltpu.VMEM((3, width, width), jnp.bfloat16),
                pltpu.VMEM((count, width), jnp.bfloat16),
                pltpu.VMEM((chunk, width), jnp.float32),
                pltpu.VMEM((width, width), jnp.float32),
                pltpu.SemaphoreType.DMA((3, shape[0], 2)),
            ],
        ),
        out_shape=[jax.ShapeDtypeStruct(shape, jnp.bfloat16)] * 2,
        cost_estimate=pl.CostEstimate(
            flops=12 * count * width * width,
            bytes_accessed=4 * count * width + 12 * width * width,
            transcendentals=count * width,
        ),
        name="gradients",
    )(core.reshape(1), token_keys, token_values, step_rates.reshape(count, 1), mine, other)


def renorm(weight, gradient):
    moved = weight - gradient
    keep = jnp.sqrt(jnp.sum(weight * weight, axis=1, keepdims=True))
    return moved * keep * lax.rsqrt(jnp.sum(moved * moved, axis=1, keepdims=True) + EPS_NORM)


def finish_kernel(
    core_ref,
    temper_ref,
    own_ref,
    before_ref,
    after_ref,
    gain_ref,
    band_ref,
    mine_ref,
    other_ref,
    query_ref,
    key_ref,
    value_ref,
    o_ref,
    whole,
    projections,
    q_rows,
    k_rows,
    v_rows,
    sems,
    projection_sems,
):
    core = core_ref[0]
    span = before_ref.shape[0]
    count, width = own_ref.shape
    fetches = whole_copies(core, mine_ref, other_ref, whole, sems)
    per_matrix = len(fetches) // 3
    later = [
        pltpu.make_async_copy(source, projections.at[i], projection_sems.at[i])
        for i, source in enumerate((key_ref, value_ref, query_ref))
    ]
    for copy in fetches + later:
        copy.start()

    def wait_for(matrix):
        for copy in fetches[matrix * per_matrix : (matrix + 1) * per_matrix]:
            copy.wait()

    band = band_ref[...]
    tile = band.shape[0]

    def head_norm(normed, matrix):
        projected = jnp.dot(normed, projections[matrix], preferred_element_type=jnp.float32)
        parts = []
        for start in range(0, width, tile):
            part = projected[:, start : start + tile]
            parts.append(part * lax.rsqrt(dot_split(part * part, band) + EPS_NORM))
        return jnp.concatenate(parts, axis=1).astype(jnp.bfloat16)

    def apply(tokens, first):
        if first:
            wait_for(0)
        pre_gate = dot_rows(tokens, whole[0])
        if first:
            wait_for(1)
        pre_up = dot_rows(tokens, whole[1])
        mixed = (pre_gate * jax.nn.sigmoid(pre_gate) * pre_up).astype(jnp.bfloat16)
        if first:
            wait_for(2)
        fast_out = dot_rows(mixed, whole[2])
        inverse = lax.rsqrt(jnp.mean(fast_out * fast_out, axis=1, keepdims=True) + EPS_NORM)
        return (fast_out * inverse * gain_ref[...]).astype(jnp.bfloat16)

    normed = apply(own_ref[...], True)
    for copy in later:
        copy.wait()
    q_rows[...] = head_norm(normed, 2)
    k_rows[span : span + count, :] = head_norm(normed, 0)
    v_rows[span : span + count, :] = jnp.dot(
        normed, projections[1], preferred_element_type=jnp.float32
    ).astype(jnp.bfloat16)

    normed = apply(jnp.concatenate([before_ref[...], after_ref[...]], axis=0), False)
    keys = head_norm(normed, 0)
    k_rows[:span, :] = keys[:span]
    k_rows[span + count :, :] = keys[span:]
    values = jnp.dot(normed, projections[1], preferred_element_type=jnp.float32).astype(
        jnp.bfloat16
    )
    v_rows[:span, :] = values[:span]
    v_rows[span + count :, :] = values[span:]

    heads = temper_ref.shape[0]
    lanes = 2 * width // heads
    size = lanes // 2
    block = 128
    reach = block + 2 * span
    left = lax.broadcasted_iota(jnp.int32, (block, lanes), 1) < size
    ahead = lax.broadcasted_iota(jnp.int32, (block, block), 1) - lax.broadcasted_iota(
        jnp.int32, (block, block), 0
    )
    ones = jnp.ones((reach, lanes), jnp.bfloat16)

    def head_pair(pair, carry):
        at = pl.ds(pl.multiple_of(pair * lanes, lanes), lanes)
        for start in range(0, count, block):
            queries = q_rows[start : start + block, at]
            zero = jnp.zeros_like(queries)
            both = jnp.concatenate(
                [jnp.where(left, queries, zero), jnp.where(left, zero, queries)], axis=0
            )
            scores = dot_rows(both, k_rows[start : start + reach, at])
            weights = []
            for head in range(2):
                mine = scores[head * block : (head + 1) * block]
                mine = jnp.concatenate(
                    [
                        jnp.where(ahead >= 0, mine[:, :block], -1e30),
                        mine[:, block : reach - block],
                        jnp.where(ahead <= 0, mine[:, reach - block :], -1e30),
                    ],
                    axis=1,
                )
                scale = temper_ref[2 * pair + head] * (1.0 / math.sqrt(size) / math.log(2.0))
                highest = jnp.max(mine, axis=1, keepdims=True)
                weights.append(jnp.exp2((mine - highest) * scale).astype(jnp.bfloat16))
            found = jnp.dot(
                jnp.concatenate(weights, axis=0),
                jnp.concatenate([v_rows[start : start + reach, at], ones], axis=1),
                preferred_element_type=jnp.float32,
            )
            result = found[:, :lanes] / found[:, lanes:]
            o_ref[start : start + block, at] = jnp.where(
                left, result[:block], result[block:]
            ).astype(jnp.bfloat16)
        return carry

    lax.fori_loop(0, heads // 2, head_pair, 0)


def finish(
    core,
    queries,
    before,
    after,
    mine,
    other,
    norm_gain,
    proj_query,
    proj_key,
    proj_value,
    head_temper,
):
    count, width = queries.shape
    span = before.shape[0]
    heads = head_temper.shape[0]
    extended = count + 2 * span
    tile = 4 * width // heads
    seat = jnp.arange(tile) // (width // heads)
    band = ((seat[:, None] == seat[None, :]) * (heads / width)).astype(jnp.bfloat16)
    vmem = pl.BlockSpec(memory_space=pltpu.VMEM)
    anywhere = pl.BlockSpec(memory_space=pl.ANY)
    return pl.pallas_call(
        finish_kernel,
        in_specs=[pl.BlockSpec(memory_space=pltpu.SMEM)] * 2 + [vmem] * 5 + [anywhere] * 5,
        out_specs=vmem,
        out_shape=jax.ShapeDtypeStruct((count, width), jnp.bfloat16),
        scratch_shapes=[
            pltpu.VMEM((3, width, width), jnp.bfloat16),
            pltpu.VMEM((3, width, width), jnp.bfloat16),
            pltpu.VMEM((count, width), jnp.bfloat16),
            pltpu.VMEM((extended, width), jnp.bfloat16),
            pltpu.VMEM((extended, width), jnp.bfloat16),
            pltpu.SemaphoreType.DMA((3, mine.shape[0], 2)),
            pltpu.SemaphoreType.DMA((3,)),
        ],
        cost_estimate=pl.CostEstimate(
            flops=12 * extended * width * width,
            bytes_accessed=12 * width * width + 6 * extended * width,
            transcendentals=count * heads * extended,
        ),
        name="finish",
    )(
        core.reshape(1),
        head_temper,
        queries,
        before,
        after,
        norm_gain.reshape(1, width),
        band,
        mine,
        other,
        proj_query,
        proj_key,
        proj_value,
    )


def per_device(
    token_keys,
    token_values,
    token_queries,
    step_rates,
    fast_gate,
    fast_up,
    fast_down,
    norm_gain,
    proj_query,
    proj_key,
    proj_value,
    head_temper,
):
    row, col = lax.axis_index("row"), lax.axis_index("col")
    x, y = (row // 2) % NX, row // (2 * NX)
    z_hi, core = col // 2, col % 2
    width = token_keys.shape[1]
    shard = fast_gate.shape[0]
    piece = 3 * shard // 4

    core_swap = pairs(lambda x, y, z, c: (x, y, z, 1 - c))
    z_four = groups(lambda x, y, z, c: ((x, y, z % 2, c), z))
    z_eight = groups(lambda x, y, z, c: ((x, y, c), z))
    mixed_four = groups(
        lambda x, y, z, c: (("y", x, z, c), y) if c == 0 else (("x", y, z, c), x)
    )
    xy_sixteen = groups(lambda x, y, z, c: ((z, c), x * NY + y))

    owned = jnp.concatenate([fast_gate, fast_up, fast_down], axis=0)
    owned_b = owned.astype(jnp.bfloat16)
    part = jnp.where(core == 0, y, x)
    mine = lax.dynamic_slice_in_dim(owned_b, part * piece, piece, 0)
    quarter = exchange(spread(mine, 4).reshape(4 * piece, width), z_four)
    half = exchange(spread(quarter, 4).reshape(16 * piece, width), mixed_four)
    half = half.reshape(4, 4, piece, width).transpose(1, 0, 2, 3).reshape(4, 3, shard, width)
    other = lax.ppermute(half, ALL, core_swap)
    other, held, queries = lax.optimization_barrier((other, owned, token_queries))

    held = lax.dynamic_slice_in_dim(held, y * piece, piece, 0)
    wide = jnp.where(z_hi == x, held, 0.0)
    for step in range(1, 4):
        sends = [
            (device_of(x, y, 2 * x + low, c), device_of(x, y, 2 * (x + step) + low, c))
            for x in range(NX)
            for y in range(NY)
            for low in range(2)
            for c in range(2)
        ]
        wide = wide + lax.ppermute(held, ALL, sends)

    count = lax.axis_size("row") * lax.axis_size("col")
    span = token_queries.shape[0] // 2
    before = lax.ppermute(queries[span:], ALL, [(i, (i + 1) % count) for i in range(count)])
    after = lax.ppermute(queries[:span], ALL, [((i + 1) % count, i) for i in range(count)])

    keep, give = gradients(core, token_keys, token_values, step_rates, half, other)
    give, before, after, wide = lax.optimization_barrier((give, before, after, wide))
    taken = lax.ppermute(give, ALL, core_swap)
    chip_sum = (keep.astype(jnp.float32) + taken.astype(jnp.float32)).astype(jnp.bfloat16)
    shares = exchange(chip_sum.reshape(16 * piece, width), xy_sixteen)
    plane = jnp.sum(shares.reshape(16, piece, width).astype(jnp.float32), axis=0)
    stack = exchange(
        spread(plane.astype(jnp.bfloat16), NZ).reshape(NZ * piece, width), z_eight
    )
    total = jnp.sum(stack.reshape(NZ, piece, width).astype(jnp.float32), axis=0)

    new_rows = renorm(wide, total).astype(jnp.bfloat16)
    half_new = exchange(spread(new_rows, 16).reshape(16 * piece, width), xy_sixteen)
    half_new = half_new.reshape(4, 3, shard, width)
    other_new = lax.ppermute(half_new, ALL, core_swap)
    own_new = lax.dynamic_index_in_dim(half_new, z_hi, 0, False).astype(jnp.float32)
    new_gate, new_up, new_down = own_new[0], own_new[1], own_new[2]

    attended = finish(
        core,
        token_queries,
        before,
        after,
        half_new,
        other_new,
        norm_gain,
        proj_query,
        proj_key,
        proj_value,
        head_temper,
    )
    return (attended, new_gate, new_up, new_down)


def solution(mesh):
    placed = (
        P(("row", "col"), None),
        P(("row", "col"), None),
        P(("row", "col"), None),
        P(("row", "col")),
        P("col", None),
        P("col", None),
        P("col", None),
        P(),
        P(),
        P(),
        P(),
        P(),
    )
    return jax.shard_map(
        per_device,
        mesh=mesh,
        in_specs=placed,
        out_specs=(P(("row", "col"), None), P("col", None), P("col", None), P("col", None)),
        check_vma=False,
    )
```
